32 devices in a mesh: gossip: 4 (over z), fsdp: 2 (over y), tensor: 4 (over x, core).
Axes of the slice: x: 2, y: 2, z: 4, core: 2. Of those that a mesh axis runs over, the one named last changes fastest.
Arguments:
- hidden: bfloat16 [4, 4, 256, 4096], P('gossip', 'fsdp', None, 'tensor'), may hold values from -6 to 6
- cotangent: bfloat16 [4, 4, 256, 4096], P('gossip', 'fsdp', None, 'tensor'), may hold values from -6 to 6
- documents: int32 [4, 4, 256], P('gossip', 'fsdp'), may hold values from 0 to 7, never falling along the last dimension, each value on 1 to 128 neighbouring positions
- q_weight: float32 [4, 4096, 2048], P('gossip', 'fsdp', 'tensor'), may hold values from -0.09375 to 0.09375
- k_weight: float32 [4, 4096, 512], P('gossip', 'fsdp', 'tensor'), may hold values from -0.09375 to 0.09375
- v_weight: float32 [4, 4096, 512], P('gossip', 'fsdp', 'tensor'), may hold values from -0.09375 to 0.09375
- o_weight: float32 [4, 4096, 2048], P('gossip', 'fsdp', 'tensor'), may hold values from -0.125 to 0.125
- edge_weight: float32 [4], P('gossip'), may hold values from 0.1 to 0.45
Outputs:
- new_q_weight: float32 [4, 4096, 2048], P('gossip', 'fsdp', 'tensor')
- new_k_weight: float32 [4, 4096, 512], P('gossip', 'fsdp', 'tensor')
- new_v_weight: float32 [4, 4096, 512], P('gossip', 'fsdp', 'tensor')
- new_o_weight: float32 [4, 4096, 2048], P('gossip', 'fsdp', 'tensor')
The draws below stay inside these ranges and needn't reach their ends.
Inputs may be any that keep to these rules, and one draw needn't show every extreme that they name: `documents`: document ids never fall along a sequence; each document spans 1 to 128 positions, and some document spans exactly 128.
All inputs are finite; a program needn't handle non-finite values.
Results may differ from the reference program's by a relative error of at most 0.007.
Values may be sent and summed in bfloat16 or wider, within the bound.
No kernel may reach another device: no remote copies, remote signals or barrier semaphores. Data moves between devices by JAX's collectives and lax.ppermute only.
A program may use at most 128 MiB of HBM per device.

```python
import math
import jax
import jax.numpy as jnp
import numpy as np
from jax import lax

D = 4096
HQ = 16
HK = 4
HD = 128
SEQ = 256
NQ = 2048
NK = 512
REPLICAS = 4
SEQS = 4
N_FSDP = 2


def level_of(key, dims, split, low, largest):
    def one(position, parts):
        draws = jax.random.uniform(jax.random.fold_in(jax.random.fold_in(key, 6), position), (parts,), jnp.float32, low / len(split), largest / len(split))
        return jnp.repeat(jnp.exp(draws), dims[position] // parts).reshape((-1,) + (1,) * (len(dims) - position - 1))

    loudness = one(*split[0])
    for cut in split[1:]:
        loudness = loudness * one(*cut)
    return loudness


def split_up(amount, total, limit, skew):
    portions = [(1 << 20) // math.isqrt(standing ** skew) + 1 for standing in range(2, amount + 1)]
    spare, given = total - limit - (amount - 1), [1] * (amount - 1)
    while spare > 0:
        movable = [i for i in range(amount - 1) if given[i] < limit]
        whole, remaining = sum([portions[i] for i in movable]), spare
        for i in movable:
            more = min(limit - given[i], max(1, remaining * portions[i] // whole), spare)
            given[i] = given[i] + more
            spare = spare - more
    return np.array([limit] + given)


def uneven(stream_key, number_of, total, reach, lean):
    if number_of == 2:
        one = jax.random.randint(stream_key, (), max(1, total - reach), min(reach, total - 1) + 1)
        return jnp.stack([one, total - one])
    sizes = jnp.asarray(split_up(number_of, total, reach, lean), jnp.int32)
    pairs = (number_of - 1) // 2
    donor, sink = sizes[1:1 + 2 * pairs:2], sizes[2:2 + 2 * pairs:2]
    margin = jnp.minimum(donor - 1, reach - sink)
    moved = jax.random.randint(jax.random.fold_in(stream_key, 1), (pairs,), 0, 1 << 20) % (margin + 1)
    sizes = sizes.at[1:1 + 2 * pairs:2].set(donor - moved).at[2:2 + 2 * pairs:2].set(sink + moved)
    return sizes[jax.random.permutation(jax.random.fold_in(stream_key, 2), number_of)]


def normal_values(own_key, dims, width, reach, pieces=(), kind=jnp.bfloat16):
    result = width * jax.random.normal(own_key, dims, jnp.float32)
    if pieces:
        result = result * level_of(own_key, dims, pieces, -0.22, 0.18)
    return jnp.clip(result, -reach, reach).astype(kind)


def setup_inputs(seed: int = 0) -> dict:
    seeds = jax.random.split(jax.random.key(seed), 9)
    return {
        "hidden": normal_values(seeds[0], (REPLICAS, SEQS, SEQ, D), 1.0, 6.0, ((0, 4), (1, 2), (3, 4))),
        "cotangent": normal_values(seeds[1], (REPLICAS, SEQS, SEQ, D), 1.0, 6.0, ((0, 4), (1, 2), (3, 4))),
        "documents": jax.vmap(lambda own: jnp.searchsorted(jnp.cumsum(uneven(own, 8, SEQ, SEQ // 2, 0)), jnp.arange(SEQ), side="right"))(jax.random.split(seeds[2], REPLICAS * SEQS)).reshape((REPLICAS, SEQS, SEQ)).astype(jnp.int32),
        "q_weight": normal_values(seeds[3], (REPLICAS, D, NQ), D ** -0.5, 0.09375, ((0, 4), (1, 2), (2, 4)), jnp.float32),
        "k_weight": normal_values(seeds[4], (REPLICAS, D, NK), D ** -0.5, 0.09375, ((0, 4), (1, 2), (2, 4)), jnp.float32),
        "v_weight": normal_values(seeds[5], (REPLICAS, D, NK), D ** -0.5, 0.09375, ((0, 4), (1, 2), (2, 4)), jnp.float32),
        "o_weight": normal_values(seeds[6], (REPLICAS, D, NQ), NQ ** -0.5, 0.125, ((0, 4), (1, 2), (2, 4)), jnp.float32),
        "edge_weight": jnp.clip(0.1 + 0.35 * jax.random.uniform(seeds[7], (REPLICAS,), jnp.float32) ** level_of(seeds[7], (REPLICAS,), ((0, 4),), -0.2, 0.2), 0.1, 0.45),
    }


rope_theta = 500000.0
learn_rate = 0.001
norm_eps = 1e-05

def contract(form, left, right):
    return jnp.einsum(form, left.astype(jnp.float32), right.astype(jnp.float32))

def rope_tables(length, head_size):
    half_dim = head_size // 2
    positions = jnp.arange(length, dtype=jnp.float32)
    freqs = jnp.exp(jnp.arange(half_dim, dtype=jnp.float32) * (-2.0 / head_size * math.log(rope_theta)))
    angles = positions[:, None] * freqs[None, :]
    return (jnp.cos(angles), jnp.sin(angles))

def rotate(values, cosine, sine_table):
    half_dim = values.shape[-1] // 2
    first_half = values[..., :half_dim]
    second_half = values[..., half_dim:]
    return jnp.concatenate([first_half * cosine - second_half * sine_table, second_half * cosine + first_half * sine_table], -1)

def unrotate(values, cosine, sine_table):
    half_dim = values.shape[-1] // 2
    first_half = values[..., :half_dim]
    second_half = values[..., half_dim:]
    return jnp.concatenate([first_half * cosine + second_half * sine_table, second_half * cosine - first_half * sine_table], -1)

def attention_grads(proj, d_ctx, documents, heads_q, heads_k):
    seq_count, length = documents.shape
    group_size = heads_q // heads_k
    q_cols = heads_q * HD
    kv_cols = heads_k * HD
    cosine, sine_table = rope_tables(length, HD)
    cos_query = cosine[None, :, None, None, :]
    sin_query = sine_table[None, :, None, None, :]
    cos_key = cosine[None, :, None, :]
    sin_key = sine_table[None, :, None, :]
    query = rotate(proj[..., :q_cols].reshape(seq_count, length, heads_k, group_size, HD), cos_query, sin_query).astype(jnp.bfloat16)
    key_rot = rotate(proj[..., q_cols:q_cols + kv_cols].reshape(seq_count, length, heads_k, HD), cos_key, sin_key).astype(jnp.bfloat16)
    value_b = proj[..., q_cols + kv_cols:].reshape(seq_count, length, heads_k, HD).astype(jnp.bfloat16)
    d_out = d_ctx.reshape(seq_count, length, heads_k, group_size, HD).astype(jnp.bfloat16)
    score_scale = 1.0 / math.sqrt(HD)
    scores = contract('bqhgd,bkhd->bhgqk', query, key_rot) * score_scale
    positions = jnp.arange(length)
    causal = positions[:, None] >= positions[None, :]
    same_doc = documents[:, :, None] == documents[:, None, :]
    allowed = (causal[None] & same_doc)[:, None, None, :, :]
    exp_scores = jnp.where(allowed, jnp.exp(scores), 0.0)
    probs_f = exp_scores / lax.optimization_barrier(jnp.sum(exp_scores, -1, keepdims=True))
    probs_b = probs_f.astype(jnp.bfloat16)
    context = contract('bhgqk,bkhd->bqhgd', probs_b, value_b).astype(jnp.bfloat16)
    d_probs = contract('bqhgd,bkhd->bhgqk', d_out, value_b)
    d_value = contract('bhgqk,bqhgd->bkhd', probs_b, d_out).astype(jnp.bfloat16)
    delta_sum = lax.optimization_barrier(jnp.sum(probs_f * d_probs, -1, keepdims=True))
    d_scores = (probs_f * (d_probs - delta_sum) * score_scale).astype(jnp.bfloat16)
    d_query = contract('bhgqk,bkhd->bqhgd', d_scores, key_rot)
    d_key = contract('bhgqk,bqhgd->bkhd', d_scores, query)
    d_query = unrotate(d_query, cos_query, sin_query).astype(jnp.bfloat16)
    d_key = unrotate(d_key, cos_key, sin_key).astype(jnp.bfloat16)
    d_proj = jnp.concatenate([d_query.reshape(seq_count, length, q_cols), d_key.reshape(seq_count, length, kv_cols), d_value.reshape(seq_count, length, kv_cols)], -1)
    return (d_proj, context.reshape(seq_count, length, q_cols))

def group_product(left, right):
    model_width = left.shape[-1]
    terms = jnp.einsum('gtd,gtn->gdn', left.reshape(N_FSDP, -1, model_width).astype(jnp.float32), right.reshape(N_FSDP, -1, right.shape[-1]).astype(jnp.float32))
    rounded = lax.optimization_barrier(terms.astype(jnp.bfloat16))
    return lax.optimization_barrier(jnp.sum(rounded.astype(jnp.float32), 0))

def replica_step(hidden, cotangent, documents, q_weight, k_weight, v_weight, o_weight):
    seq_count, length, model_width = hidden.shape
    token_rows = seq_count * length
    hidden_f = hidden.reshape(token_rows, model_width).astype(jnp.float32)
    normed = (hidden_f * lax.rsqrt(lax.optimization_barrier(jnp.mean(hidden_f * hidden_f, -1, keepdims=True)) + norm_eps)).astype(jnp.bfloat16)
    cotan_rows = cotangent.reshape(token_rows, model_width)
    packed = jnp.concatenate([q_weight, k_weight, v_weight], 1).astype(jnp.bfloat16)
    proj = jnp.dot(normed, packed, preferred_element_type=jnp.float32)
    d_ctx = jnp.dot(cotan_rows, o_weight.astype(jnp.bfloat16), preferred_element_type=jnp.float32)
    d_proj, context = attention_grads(proj.reshape(seq_count, length, -1), d_ctx.reshape(seq_count, length, -1), documents, HQ, HK)
    grad_proj = group_product(normed, d_proj.reshape(token_rows, -1))
    grad_out = group_product(cotan_rows, context.reshape(token_rows, -1))
    q_cols = HQ * HD
    kv_cols = HK * HD
    return (q_weight - learn_rate * grad_proj[:, :q_cols], k_weight - learn_rate * grad_proj[:, q_cols:q_cols + kv_cols], v_weight - learn_rate * grad_proj[:, q_cols + kv_cols:], o_weight - learn_rate * grad_out)

def reference(hidden, cotangent, documents, q_weight, k_weight, v_weight, o_weight, edge_weight):

    def one_replica(packed_args):
        return replica_step(*packed_args)
    updated = lax.map(one_replica, (hidden, cotangent, documents, q_weight, k_weight, v_weight, o_weight))
    c_low = jnp.roll(edge_weight, 1)[:, None, None]
    c_high = edge_weight[:, None, None]
    new_weights = []
    for weights in updated:
        from_low = jnp.roll(weights, 1, axis=0)
        from_high = jnp.roll(weights, -1, axis=0)
        new_weights.append(weights + c_low * (from_low - weights) + c_high * (from_high - weights))
    return (new_weights[0], new_weights[1], new_weights[2], new_weights[3])
```

```python
import functools
import math

import jax
import jax.numpy as jnp
from jax import lax
from jax.experimental import pallas as pl
from jax.experimental.pallas import tpu as pltpu
from jax.sharding import PartitionSpec as P

HD = 128
F32 = jnp.float32
BF16 = jnp.bfloat16
BLOCK = 256

rope_theta = 500000.0
learn_rate = 0.001
norm_eps = 1e-05

NN = (((1,), (0,)), ((), ()))
NT = (((1,), (1,)), ((), ()))
TN = (((0,), (0,)), ((), ()))


def mm(left, right, form=NN):
    return lax.dot_general(left, right, form, preferred_element_type=F32)


def cost(flops, bytes_accessed, transcendentals=0):
    return pl.CostEstimate(
        flops=int(flops), bytes_accessed=int(bytes_accessed), transcendentals=int(transcendentals)
    )


def params(count):
    return pltpu.CompilerParams(
        dimension_semantics=("arbitrary",) * count, vmem_limit_bytes=40 * 1024 * 1024
    )


def passed_along(shard, axis, by):
    count = lax.axis_size(axis)
    return lax.ppermute(shard, axis, [(i, (i + by) % count) for i in range(count)])


def rope_tables(length, head_size):
    half_dim = head_size // 2
    positions = jnp.arange(length, dtype=F32)
    freqs = jnp.exp(jnp.arange(half_dim, dtype=F32) * (-2.0 / head_size * math.log(rope_theta)))
    angles = positions[:, None] * freqs[None, :]
    cosine, sine = jnp.cos(angles), jnp.sin(angles)
    return jnp.concatenate([cosine, cosine], 1), jnp.concatenate([-sine, sine], 1)


def after(value, *others):
    return lax.optimization_barrier((value, *others))[0]


def spread(shard, fsdp_count, tensor_count):
    share = tensor_count // fsdp_count
    near, far = [], []
    for g in range(fsdp_count):
        for t in range(tensor_count):
            x, lane = divmod(t, share)
            source = g * tensor_count + t
            across = x * tensor_count + (1 - x) * share + lane
            if x == g:
                near.append((source, across))
            else:
                near.append((source, x * tensor_count + t))
                far.append((source, across))
    axes = ("fsdp", "tensor")
    return lax.ppermute(shard, axes, near), lax.ppermute(shard, axes, far)


def swapped(block, tensor_count):
    return lax.ppermute(block, "tensor", [(t, t ^ 1) for t in range(tensor_count)])


def parity_halves(par_ref, w_ref, rows):
    par = par_ref[0]
    return (
        w_ref[pl.ds(pl.multiple_of(par * rows, rows), rows), :],
        w_ref[pl.ds(pl.multiple_of((1 - par) * rows, rows), rows), :],
    )


def project_kernel(par_ref, *refs):
    *pieces, w_ref, own_ref, oth_ref, sent_ref = refs
    _, tokens, rows = pieces[0].shape
    w_mine, w_theirs = parity_halves(par_ref, w_ref, rows)
    for part in range(len(pieces) // 2):
        mine, theirs = pieces[2 * part : 2 * part + 2]
        at = pl.ds(part * tokens, tokens)
        other = mm(mine[1], w_mine) + mm(theirs[1], w_theirs)
        sent_ref[at, :] = other.astype(BF16)
        oth_ref[at, :] = other
        own_ref[at, :] = mm(mine[0], w_mine) + mm(theirs[0], w_theirs)


def project(par, pieces, weight, at, cols):
    parts = len(pieces) // 2
    _, tokens, rows = pieces[0].shape
    if parts == 1:
        steps, unit = 2, cols
        piece = pl.BlockSpec((2, tokens // steps, rows), lambda i, p: (0, i, 0))
        whole = pl.BlockSpec((2 * rows, cols), lambda i, p: (0, at))
        out = pl.BlockSpec((tokens // steps, cols), lambda i, p: (i, 0))
    else:
        unit = 2 * HD
        steps = cols // unit
        piece = pl.BlockSpec((2, tokens, rows), lambda i, p: (0, 0, 0))
        whole = pl.BlockSpec((2 * rows, unit), lambda i, p: (0, at * steps + i))
        out = pl.BlockSpec((parts * tokens, unit), lambda i, p: (0, i))
    tokens = tokens * parts
    return pl.pallas_call(
        project_kernel,
        grid_spec=pltpu.PrefetchScalarGridSpec(
            num_scalar_prefetch=1,
            grid=(steps,),
            in_specs=[piece] * len(pieces) + [whole],
            out_specs=[out] * 3,
        ),
        out_shape=[jax.ShapeDtypeStruct((tokens, cols), kind) for kind in (F32, F32, BF16)],
        compiler_params=params(1),
        cost_estimate=cost(8 * tokens * rows * cols, 8 * tokens * rows + 10 * tokens * cols),
        name="project",
    )(par, *pieces, weight)


def rotated(values, cos, sin):
    return values * cos + pltpu.roll(values, HD // 2, 1) * sin


def unrotated(values, cos, sin):
    return values * cos - pltpu.roll(values, HD // 2, 1) * sin


def probabilities(query, key, mask):
    scores = mm(query, key, NT) * (1.0 / math.sqrt(HD))
    exp_scores = jnp.where(mask, jnp.exp(scores), 0.0)
    return exp_scores / jnp.sum(exp_scores, -1, keepdims=True)


def first_kernel(own, oth, cos, sin, mask, q_ref, k_ref, v_ref, ctx_ref):
    proj = own[...] + oth[...].astype(F32)
    key = rotated(proj[:, :HD], cos[...], sin[...]).astype(BF16)
    value = proj[:, HD : 2 * HD].astype(BF16)
    query = rotated(proj[:, 2 * HD :], cos[...], sin[...]).astype(BF16)
    probs = probabilities(query, key, mask[0] > 0.5)
    ctx_ref[...] = mm(probs.astype(BF16), value).astype(BF16)
    q_ref[...] = query
    k_ref[...] = key
    v_ref[...] = value


def rest_kernel(heads, own, oth, cos, sin, mask, k_ref, v_ref, q_ref, ctx_ref):
    key, value = k_ref[...], v_ref[...]
    allowed = mask[0] > 0.5
    for head in range(heads):
        cols = slice(head * HD, (head + 1) * HD)
        proj = own[:, cols] + oth[:, cols].astype(F32)
        query = rotated(proj, cos[...], sin[...]).astype(BF16)
        probs = probabilities(query, key, allowed)
        ctx_ref[:, cols] = mm(probs.astype(BF16), value).astype(BF16)
        q_ref[:, cols] = query


def back_kernel(
    heads, own, oth, cos, sin, mask, q0_ref, q_ref, k_ref, v_ref, out_ref
):
    key, value = k_ref[...], v_ref[...]
    allowed = mask[0] > 0.5
    d_key = jnp.zeros(key.shape, F32)
    d_value = jnp.zeros(key.shape, F32)
    for head in range(heads):
        cols = slice(head * HD, (head + 1) * HD)
        query = q0_ref[...] if head == 0 else q_ref[:, (head - 1) * HD : head * HD]
        d_out = (own[:, cols] + oth[:, cols].astype(F32)).astype(BF16)
        probs = probabilities(query, key, allowed)
        d_probs = mm(d_out, value, NT)
        d_value += mm(probs.astype(BF16), d_out, TN)
        delta = jnp.sum(probs * d_probs, -1, keepdims=True)
        d_scores = (probs * (d_probs - delta) * (1.0 / math.sqrt(HD))).astype(BF16)
        d_query = unrotated(mm(d_scores, key), cos[...], sin[...])
        out_ref[:, (head + 2) * HD : (head + 3) * HD] = d_query.astype(BF16)
        d_key += mm(d_scores, query, TN)
    out_ref[:, :HD] = unrotated(d_key, cos[...], sin[...]).astype(BF16)
    out_ref[:, HD : 2 * HD] = d_value.astype(BF16)


def per_sequence(kernel, arrays, *, tables, mask, outs, name, work):
    length = tables[0].shape[0]
    seqs = mask.shape[0]

    def by_rows(cols, at=0):
        return pl.BlockSpec((length, cols), lambda s: (s, at))

    arrays = [a if isinstance(a, tuple) else (a, a.shape[1], 0) for a in arrays]
    specs = [by_rows(cols, at) for _, cols, at in arrays]
    table = pl.BlockSpec((length, HD), lambda s: (0, 0))
    values = [a for a, _, _ in arrays]
    return pl.pallas_call(
        kernel,
        grid=(seqs,),
        in_specs=specs[:2]
        + [table, table, pl.BlockSpec((1, length, length), lambda s: (s, 0, 0))]
        + specs[2:],
        out_specs=[by_rows(cols) for cols in outs],
        out_shape=[jax.ShapeDtypeStruct((seqs * length, cols), BF16) for cols in outs],
        compiler_params=params(1),
        cost_estimate=cost(
            seqs * work * length * length * HD,
            4 * seqs * length * sum(outs),
            seqs * length * length,
        ),
        name=name,
    )(*values[:2], *tables, mask, *values[2:])


def step_kernel(par_ref, *refs):
    *pieces, dy_own, dy_oth, w_mine, w_theirs, u_ref, sent_ref = refs
    cols = u_ref.shape[2]
    tokens = pieces[0].shape[1]
    at = pl.ds(pl.multiple_of(pl.program_id(1) * cols, cols), cols)
    for place, weight in ((0, w_mine), (1, w_theirs)):
        grad = 0.0
        for group, dy in ((0, dy_own), (1, dy_oth)):
            term = 0.0
            for part in range(len(pieces) // 2):
                rows = pl.ds(part * tokens, tokens)
                term += mm(pieces[2 * part + place][group], dy[rows, at], TN)
            grad += term.astype(BF16).astype(F32)
        updated = weight[...] - learn_rate * grad
        u_ref[place] = updated
        sent_ref[place] = updated.astype(BF16)


def step_weights(par, pieces, d_own, d_oth, weight, first_col, unit, blocks=None):
    _, part_tokens, rows = pieces[0].shape
    tokens, cols = d_own.shape
    total = rows // BLOCK
    begin, end = blocks or (0, total)
    count = end - begin
    at = first_col // unit
    piece = pl.BlockSpec((2, part_tokens, BLOCK), lambda j, k, p: (0, 0, begin + j))
    whole = pl.BlockSpec((tokens, cols), lambda j, k, p: (0, 0))
    out = pl.BlockSpec((2, BLOCK, unit), lambda j, k, p: (0, j, k))
    mine = lambda j, k, p: (p[0] * total + begin + j, at + k)
    theirs = lambda j, k, p: ((1 - p[0]) * total + begin + j, at + k)
    return pl.pallas_call(
        step_kernel,
        grid_spec=pltpu.PrefetchScalarGridSpec(
            num_scalar_prefetch=1,
            grid=(count, cols // unit),
            in_specs=[piece] * len(pieces)
            + [whole, whole]
            + [pl.BlockSpec((BLOCK, unit), mine), pl.BlockSpec((BLOCK, unit), theirs)],
            out_specs=[out, out],
        ),
        out_shape=[
            jax.ShapeDtypeStruct((2, count * BLOCK, cols), F32),
            jax.ShapeDtypeStruct((2, count * BLOCK, cols), BF16),
        ],
        compiler_params=params(2),
        cost_estimate=cost(8 * tokens * count * BLOCK * cols, count * BLOCK * (8 * tokens + 20 * cols)),
        name="step_weights",
    )(par, *pieces, d_own, d_oth, weight, weight)


def mix_kernel(par_ref, coef, u_ref, low_ref, high_ref, *outs):
    updated = u_ref[0]
    out_ref = outs[-1]
    out_ref[...] = (
        updated
        + coef[0] * (low_ref[0].astype(F32) - updated)
        + coef[1] * (high_ref[0].astype(F32) - updated)
    )


def mix(par, coef, chunk, rows, cols, width, to_col, begin, buffer=None):
    count = chunk[0].shape[1]
    block = min(2 * BLOCK, count)
    total, first, to = rows // block, begin * BLOCK // block, to_col // cols
    source = pl.BlockSpec((1, block, cols), lambda i, j, p: (i, j, 0))
    place = pl.BlockSpec(
        (block, cols), lambda i, j, p: ((p[0] + i * (1 - 2 * p[0])) * total + first + j, to)
    )
    extra = [] if buffer is None else [buffer]
    return pl.pallas_call(
        mix_kernel,
        grid_spec=pltpu.PrefetchScalarGridSpec(
            num_scalar_prefetch=1,
            grid=(2, count // block),
            in_specs=[pl.BlockSpec(memory_space=pltpu.SMEM), source, source, source]
            + [pl.BlockSpec(memory_space=pl.ANY)] * len(extra),
            out_specs=place,
        ),
        out_shape=jax.ShapeDtypeStruct((2 * rows, width), F32),
        input_output_aliases={5: 0} if extra else {},
        compiler_params=params(2),
        cost_estimate=cost(10 * count * cols, 24 * count * cols),
        name="mix",
    )(par, coef, *chunk, *extra)


def body(fsdp_count, tensor_count, hidden, cotangent, documents, q_w, k_w, v_w, o_w, edge_weight):
    _, seqs, length, shard_cols = hidden.shape
    tokens = seqs * length
    model_width = shard_cols * tensor_count
    q_cols = q_w.shape[2]
    heads = q_cols // HD
    tensor_at, fsdp_at = lax.axis_index("tensor"), lax.axis_index("fsdp")
    share = tensor_count // fsdp_count
    home = tensor_at // share == fsdp_at
    par = (tensor_at % share).astype(jnp.int32).reshape(1)
    other = functools.partial(passed_along, axis="fsdp", by=1)
    flip = lambda block: swapped(block, tensor_count)
    far_flip = lambda block: lax.ppermute(
        block, "tensor", [(t, (t + share) % tensor_count) for t in range(tensor_count)]
    )

    shard = hidden[0].reshape(tokens, shard_cols)
    cotan = cotangent[0].reshape(tokens, shard_cols)
    h_near, h_far = spread(shard, fsdp_count, tensor_count)

    coef = jnp.concatenate([passed_along(edge_weight, "gossip", 1), edge_weight])

    wide = shard.astype(F32)
    squares = jnp.sum(wide * wide, -1)
    got = flip(squares)
    wq, wk, wv = after((q_w[0], k_w[0], v_w[0]), squares)
    squares = squares + got
    got_x = far_flip(squares)
    docs = documents[0].astype(F32)
    got_y = other(jnp.concatenate([squares, docs.reshape(tokens)]))
    got_xy = lax.ppermute(
        squares,
        ("fsdp", "tensor"),
        [
            (g * tensor_count + t, (1 - g) * tensor_count + (t + share) % tensor_count)
            for g in range(fsdp_count)
            for t in range(tensor_count)
        ],
    )
    w_proj = jnp.concatenate(after((wk, wv, wq), squares), 1).astype(BF16)
    w_out = after(o_w[0], squares).astype(BF16)
    tables = rope_tables(length, HD)
    positions = jnp.arange(length)
    causal = (positions[:, None] >= positions[None, :])[None]

    def mask_of(docs):
        docs = after(docs, squares)
        return (causal & (docs[:, :, None] == docs[:, None, :])).astype(F32)

    mask = mask_of(docs)
    got_x, coef, w_proj, w_out, mask, *tables = lax.optimization_barrier(
        (got_x, coef, w_proj, w_out, mask, *tables)
    )
    inv_own = lax.rsqrt((squares + got_x) / model_width + norm_eps)
    inv_oth = lax.rsqrt((got_y[:tokens] + got_xy) / model_width + norm_eps)

    def pieces_of(part, near, far, scale_own=None, scale_oth=None):
        own = jnp.where(home, part, near)
        oth = jnp.where(home, near, far)
        if scale_own is not None:
            own = (own.astype(F32) * scale_own[:, None]).astype(BF16)
            oth = (oth.astype(F32) * scale_oth[:, None]).astype(BF16)
        mine = lax.optimization_barrier(jnp.stack([own, oth]))
        return mine, flip(mine)

    c_near, c_far = spread(after(cotan, h_near, h_far), fsdp_count, tensor_count)
    h_pieces = pieces_of(shard, h_near, h_far, inv_own, inv_oth)
    first_cols, rest_cols = 3 * HD, q_cols - HD
    first_own, first_oth, first_sent = project(par, h_pieces, w_proj, 0, first_cols)
    first_sent = jnp.concatenate([first_sent, first_own.astype(BF16)], 1)
    first_got = other(first_sent)
    rest_own, rest_oth, rest_sent = project(par, after(h_pieces, first_sent), w_proj, 1, rest_cols)
    rest_sent = jnp.concatenate([rest_sent, rest_own.astype(BF16)], 1)
    mask_oth = mask_of(after(got_y[tokens:], rest_sent).reshape(docs.shape))
    c_near, c_far = after((c_near, c_far), rest_sent, mask_oth)
    c_pieces = pieces_of(cotan, c_near, c_far)
    first_got = after(first_got, c_pieces[0])
    first = functools.partial(
        per_sequence, first_kernel, tables=tables, outs=(HD,) * 4, name="first_head", work=4
    )
    q0, key, value, ctx0 = first((first_own, (first_got, first_cols, 0)), mask=mask)
    q0_oth, key_oth, value_oth, ctx0_oth = first(
        (first_oth, (first_got, first_cols, 1)), mask=mask_oth
    )
    rest_got = other(after(rest_sent, first_got))

    def shared(pair, *gates):
        updated, sent = pair
        sent = after(sent, *gates) if gates else sent
        return updated, passed_along(sent, "gossip", 1), passed_along(sent, "gossip", -1)

    o_step = functools.partial(step_weights, par, c_pieces)
    blocks = shard_cols // BLOCK
    z1 = shared(o_step(ctx0, ctx0_oth, o_w[0], 0, HD, (0, blocks // 2)))
    z2 = shared(o_step(after(ctx0, z1[0]), ctx0_oth, o_w[0], 0, HD, (blocks // 2, blocks)))
    d_own, d_oth, d_sent = project(par, after(c_pieces, z2[0]), w_out, 0, q_cols)
    d_sent = jnp.concatenate([d_sent, d_own.astype(BF16)], 1)
    rest_got = after(rest_got, d_sent, *z1[1:])
    d_got = other(after(d_sent, rest_got))
    rest = functools.partial(
        per_sequence,
        functools.partial(rest_kernel, heads - 1),
        tables=tables,
        outs=(rest_cols,) * 2,
        name="rest_heads",
        work=4 * (heads - 1),
    )
    q_rest, ctx_rest = rest((rest_own, (rest_got, rest_cols, 0), key, value), mask=mask)
    q_rest_oth, ctx_rest_oth = rest(
        (rest_oth, (rest_got, rest_cols, 1), key_oth, value_oth), mask=mask_oth
    )
    chunks = [z1, z2]
    for i in range(heads - 1):
        at = slice(i * HD, (i + 1) * HD)
        d_ctx = after(ctx_rest[:, at], chunks[-1][0])
        chunks.append(shared(o_step(d_ctx, ctx_rest_oth[:, at], o_w[0], (i + 1) * HD, HD)))
    d_got = after(d_got, chunks[-1][0])
    back = functools.partial(
        per_sequence,
        functools.partial(back_kernel, heads),
        tables=tables,
        outs=(q_cols + 2 * HD,),
        name="attention_back",
        work=14 * heads,
    )
    d_proj = back((d_own, (d_got, q_cols, 0), q0, q_rest, key, value), mask=mask)[0]
    d_proj_oth = back(
        (d_oth, (d_got, q_cols, 1), q0_oth, q_rest_oth, key_oth, value_oth), mask=mask_oth
    )[0]
    h_step = functools.partial(step_weights, par, h_pieces)
    half = q_cols // 2
    for weight, first_col, begin, cols in (
        (k_w[0], 0, 0, HD),
        (v_w[0], 0, HD, HD),
        (q_w[0], 0, 2 * HD, half),
        (q_w[0], half, 2 * HD + half, half),
    ):
        at = slice(begin, begin + cols)
        d_own = after(d_proj[:, at], chunks[-1][0])
        chunks.append(shared(h_step(d_own, d_proj_oth[:, at], weight, first_col, cols)))

    outs = {}
    last = coef
    for chunk, (name, cols, width, first_col) in zip(
        chunks,
        [("o", HD, q_cols, max(i, 0) * HD) for i in range(-1, heads)]
        + [("k", HD, HD, 0), ("v", HD, HD, 0), ("q", half, q_cols, 0), ("q", half, q_cols, half)],
    ):
        chunk = (chunk[0], *after(chunk[1:], last))
        begin = blocks // 2 if chunk[0].shape[1] < shard_cols and name in outs else 0
        last = outs[name] = mix(
            par, coef, chunk, shard_cols, cols, width, first_col, begin, outs.get(name)
        )
    return tuple(outs[name][None] for name in "qkvo")


def solution(mesh):
    fsdp_count, tensor_count = mesh.shape["fsdp"], mesh.shape["tensor"]
    assert fsdp_count == 2 and tensor_count == 2 * fsdp_count
    activations = P("gossip", "fsdp", None, "tensor")
    weights = P("gossip", "fsdp", "tensor")
    return jax.shard_map(
        functools.partial(body, fsdp_count, tensor_count),
        mesh=mesh,
        in_specs=(activations, activations, P("gossip", "fsdp", None))
        + (weights,) * 4
        + (P("gossip"),),
        out_specs=(weights,) * 4,
        check_vma=False,
    )
```

```python
import functools
import math

import jax
import jax.numpy as jnp
from jax import lax
from jax.experimental import pallas as pl
from jax.experimental.pallas import tpu as pltpu
from jax.sharding import PartitionSpec as P

HD = 128
F32 = jnp.float32
BF16 = jnp.bfloat16
BLOCK = 256
CORE_PARTS = 4
VMEM_LIMIT = 24 * 1024 * 1024

rope_theta = 500000.0
learn_rate = 0.001
norm_eps = 1e-05

NN = (((1,), (0,)), ((), ()))
NT = (((1,), (1,)), ((), ()))
TN = (((0,), (0,)), ((), ()))


def mm(left, right, form=NN):
    return lax.dot_general(left, right, form, preferred_element_type=F32)


def cost(flops, bytes_accessed, transcendentals=0):
    return pl.CostEstimate(
        flops=int(flops), bytes_accessed=int(bytes_accessed), transcendentals=int(transcendentals)
    )


def params(count):
    return pltpu.CompilerParams(
        dimension_semantics=("arbitrary",) * count, vmem_limit_bytes=VMEM_LIMIT
    )


def passed_along(shard, axis, by):
    count = lax.axis_size(axis)
    return lax.ppermute(shard, axis, [(i, (i + by) % count) for i in range(count)])


def rope_tables(length, head_size):
    half_dim = head_size // 2
    positions = jnp.arange(length, dtype=F32)
    freqs = jnp.exp(jnp.arange(half_dim, dtype=F32) * (-2.0 / head_size * math.log(rope_theta)))
    angles = positions[:, None] * freqs[None, :]
    cosine, sine = jnp.cos(angles), jnp.sin(angles)
    return jnp.concatenate([cosine, cosine], 1), jnp.concatenate([-sine, sine], 1)


def after(value, *others):
    return lax.optimization_barrier((value, *others))[0]


def spread(shard, fsdp_count, tensor_count):
    share = tensor_count // fsdp_count
    near, far = [], []
    for g in range(fsdp_count):
        for t in range(tensor_count):
            x, lane = divmod(t, share)
            source = g * tensor_count + t
            across = x * tensor_count + (1 - x) * share + lane
            if x == g:
                near.append((source, across))
            else:
                near.append((source, x * tensor_count + t))
                far.append((source, across))
    axes = ("fsdp", "tensor")
    return lax.ppermute(shard, axes, near), lax.ppermute(shard, axes, far)


def swapped(block, tensor_count):
    return lax.ppermute(block, "tensor", [(t, t ^ 1) for t in range(tensor_count)])


def parity_halves(par_ref, w_ref, rows):
    par = par_ref[0]
    return (
        w_ref[pl.ds(pl.multiple_of(par * rows, rows), rows), :],
        w_ref[pl.ds(pl.multiple_of((1 - par) * rows, rows), rows), :],
    )


def project_kernel(par_ref, *refs):
    *pieces, w_ref, own_ref, oth_ref, sent_ref = refs
    _, tokens, rows = pieces[0].shape
    w_mine, w_theirs = parity_halves(par_ref, w_ref, rows)
    for part in range(len(pieces) // 2):
        mine, theirs = pieces[2 * part : 2 * part + 2]
        at = pl.ds(part * tokens, tokens)
        other = mm(mine[1], w_mine) + mm(theirs[1], w_theirs)
        sent_ref[0, at, :] = other.astype(BF16)
        oth_ref[at, :] = other
        own = mm(mine[0], w_mine) + mm(theirs[0], w_theirs)
        sent_ref[1, at, :] = own.astype(BF16)
        own_ref[at, :] = own


def project(par, pieces, weight, at, cols):
    parts = len(pieces) // 2
    _, tokens, rows = pieces[0].shape
    if parts == 1:
        steps, unit = 2, cols
        piece = pl.BlockSpec((2, tokens // steps, rows), lambda i, p: (0, i, 0))
        whole = pl.BlockSpec((2 * rows, cols), lambda i, p: (0, at))
        out = pl.BlockSpec((tokens // steps, cols), lambda i, p: (i, 0))
        sent = pl.BlockSpec((2, tokens // steps, cols), lambda i, p: (0, i, 0))
    else:
        unit = 2 * HD
        steps = cols // unit
        piece = pl.BlockSpec((2, tokens, rows), lambda i, p: (0, 0, 0))
        whole = pl.BlockSpec((2 * rows, unit), lambda i, p: (0, at * steps + i))
        out = pl.BlockSpec((parts * tokens, unit), lambda i, p: (0, i))
        sent = pl.BlockSpec((2, parts * tokens, unit), lambda i, p: (0, 0, i))
    tokens = tokens * parts
    return pl.pallas_call(
        project_kernel,
        grid_spec=pltpu.PrefetchScalarGridSpec(
            num_scalar_prefetch=1,
            grid=(steps,),
            in_specs=[piece] * len(pieces) + [whole],
            out_specs=[out, out, sent],
        ),
        out_shape=[jax.ShapeDtypeStruct((tokens, cols), F32)] * 2
        + [jax.ShapeDtypeStruct((2, tokens, cols), BF16)],
        compiler_params=params(1),
        cost_estimate=cost(8 * tokens * rows * cols, 8 * tokens * rows + 10 * tokens * cols),
        name="project",
    )(par, *pieces, weight)


def rotated(values, cos, sin):
    return values * cos + pltpu.roll(values, HD // 2, 1) * sin


def unrotated(values, cos, sin):
    return values * cos - pltpu.roll(values, HD // 2, 1) * sin


def probabilities(query, key, mask):
    scores = mm(query, key, NT) * (1.0 / math.sqrt(HD))
    exp_scores = jnp.where(mask, jnp.exp(scores), 0.0)
    return exp_scores / jnp.sum(exp_scores, -1, keepdims=True)


def first_kernel(own, oth, cos, sin, mask, q_ref, k_ref, v_ref, ctx_ref):
    proj = own[...] + oth[...].astype(F32)
    key = rotated(proj[:, :HD], cos[...], sin[...]).astype(BF16)
    value = proj[:, HD : 2 * HD].astype(BF16)
    query = rotated(proj[:, 2 * HD :], cos[...], sin[...]).astype(BF16)
    probs = probabilities(query, key, mask[0] > 0.5)
    ctx_ref[...] = mm(probs.astype(BF16), value).astype(BF16)
    q_ref[...] = query
    k_ref[...] = key
    v_ref[...] = value


def rest_kernel(heads, own, oth, cos, sin, mask, k_ref, v_ref, q_ref, ctx_ref):
    key, value = k_ref[...], v_ref[...]
    allowed = mask[0] > 0.5
    for head in range(heads):
        cols = slice(head * HD, (head + 1) * HD)
        proj = own[:, cols] + oth[:, cols].astype(F32)
        query = rotated(proj, cos[...], sin[...]).astype(BF16)
        probs = probabilities(query, key, allowed)
        ctx_ref[:, cols] = mm(probs.astype(BF16), value).astype(BF16)
        q_ref[:, cols] = query


def back_kernel(
    heads, own, oth, cos, sin, mask, q0_ref, q_ref, k_ref, v_ref, out_ref
):
    key, value = k_ref[...], v_ref[...]
    allowed = mask[0] > 0.5
    d_key = jnp.zeros(key.shape, F32)
    d_value = jnp.zeros(key.shape, F32)
    for head in range(heads):
        cols = slice(head * HD, (head + 1) * HD)
        query = q0_ref[...] if head == 0 else q_ref[:, (head - 1) * HD : head * HD]
        d_out = (own[:, cols] + oth[:, cols].astype(F32)).astype(BF16)
        probs = probabilities(query, key, allowed)
        d_probs = mm(d_out, value, NT)
        d_value += mm(probs.astype(BF16), d_out, TN)
        delta = jnp.sum(probs * d_probs, -1, keepdims=True)
        d_scores = (probs * (d_probs - delta) * (1.0 / math.sqrt(HD))).astype(BF16)
        d_query = unrotated(mm(d_scores, key), cos[...], sin[...])
        out_ref[:, (head + 2) * HD : (head + 3) * HD] = d_query.astype(BF16)
        d_key += mm(d_scores, query, TN)
    out_ref[:, :HD] = unrotated(d_key, cos[...], sin[...]).astype(BF16)
    out_ref[:, HD : 2 * HD] = d_value.astype(BF16)


def per_sequence(kernel, arrays, *, tables, mask, outs, name, work):
    length = tables[0].shape[0]
    seqs = mask.shape[0]

    def by_rows(array):
        if isinstance(array, tuple):
            array, at = array
            return pl.BlockSpec((None, length, array.shape[2]), lambda s: (at, s, 0))
        return pl.BlockSpec((length, array.shape[1]), lambda s: (s, 0))

    specs = [by_rows(a) for a in arrays]
    values = [a[0] if isinstance(a, tuple) else a for a in arrays]
    table = pl.BlockSpec((length, HD), lambda s: (0, 0))
    return pl.pallas_call(
        kernel,
        grid=(seqs,),
        in_specs=specs[:2]
        + [table, table, pl.BlockSpec((1, length, length), lambda s: (s, 0, 0))]
        + specs[2:],
        out_specs=[pl.BlockSpec((length, cols), lambda s: (s, 0)) for cols in outs],
        out_shape=[jax.ShapeDtypeStruct((seqs * length, cols), BF16) for cols in outs],
        compiler_params=params(1),
        cost_estimate=cost(
            seqs * work * length * length * HD,
            4 * seqs * length * sum(outs),
            seqs * length * length,
        ),
        name=name,
    )(*values[:2], *tables, mask, *values[2:])


def step_kernel(par_ref, *refs):
    *pieces, dy_own, dy_oth, w_mine, w_theirs, u_ref, sent_ref = refs
    cols = u_ref.shape[2]
    tokens = pieces[0].shape[1]
    at = pl.ds(pl.multiple_of(pl.program_id(1) * cols, cols), cols)
    for place, weight in ((0, w_mine), (1, w_theirs)):
        grad = 0.0
        for group, dy in ((0, dy_own), (1, dy_oth)):
            term = 0.0
            for part in range(len(pieces) // 2):
                rows = pl.ds(part * tokens, tokens)
                term += mm(pieces[2 * part + place][group], dy[rows, at], TN)
            grad += term.astype(BF16).astype(F32)
        updated = weight[...] - learn_rate * grad
        u_ref[place] = updated
        sent_ref[place] = updated.astype(BF16)


def step_weights(par, pieces, d_own, d_oth, weight, first_col, unit, blocks=None):
    _, part_tokens, rows = pieces[0].shape
    tokens, cols = d_own.shape
    total = rows // BLOCK
    begin, end = blocks or (0, total)
    count = end - begin
    at = first_col // unit
    piece = pl.BlockSpec((2, part_tokens, BLOCK), lambda j, k, p: (0, 0, begin + j))
    whole = pl.BlockSpec((tokens, cols), lambda j, k, p: (0, 0))
    out = pl.BlockSpec((2, BLOCK, unit), lambda j, k, p: (0, j, k))
    mine = lambda j, k, p: (p[0] * total + begin + j, at + k)
    theirs = lambda j, k, p: ((1 - p[0]) * total + begin + j, at + k)
    return pl.pallas_call(
        step_kernel,
        grid_spec=pltpu.PrefetchScalarGridSpec(
            num_scalar_prefetch=1,
            grid=(count, cols // unit),
            in_specs=[piece] * len(pieces)
            + [whole, whole]
            + [pl.BlockSpec((BLOCK, unit), mine), pl.BlockSpec((BLOCK, unit), theirs)],
            out_specs=[out, out],
        ),
        out_shape=[
            jax.ShapeDtypeStruct((2, count * BLOCK, cols), F32),
            jax.ShapeDtypeStruct((2, count * BLOCK, cols), BF16),
        ],
        compiler_params=params(2),
        cost_estimate=cost(8 * tokens * count * BLOCK * cols, count * BLOCK * (8 * tokens + 20 * cols)),
        name="step_weights",
    )(par, *pieces, d_own, d_oth, weight, weight)


def mix_kernel(par_ref, coef, u_ref, low_ref, high_ref, *outs):
    updated = u_ref[0]
    out_ref = outs[-1]
    out_ref[...] = (
        updated
        + coef[0] * (low_ref[0].astype(F32) - updated)
        + coef[1] * (high_ref[0].astype(F32) - updated)
    )


def mix(par, coef, chunk, rows, cols, width, to_col, begin, buffer=None):
    count = chunk[0].shape[1]
    block = min(4 * BLOCK, count)
    total, first, to = rows // block, begin * BLOCK // block, to_col // cols
    source = pl.BlockSpec((1, block, cols), lambda i, j, p: (i, j, 0))
    place = pl.BlockSpec(
        (block, cols), lambda i, j, p: ((p[0] + i * (1 - 2 * p[0])) * total + first + j, to)
    )
    extra = [] if buffer is None else [buffer]
    return pl.pallas_call(
        mix_kernel,
        grid_spec=pltpu.PrefetchScalarGridSpec(
            num_scalar_prefetch=1,
            grid=(2, count // block),
            in_specs=[pl.BlockSpec(memory_space=pltpu.SMEM), source, source, source]
            + [pl.BlockSpec(memory_space=pl.ANY)] * len(extra),
            out_specs=place,
        ),
        out_shape=jax.ShapeDtypeStruct((2 * rows, width), F32),
        input_output_aliases={5: 0} if extra else {},
        compiler_params=params(2),
        cost_estimate=cost(10 * count * cols, 24 * count * cols),
        name="mix",
    )(par, coef, *chunk, *extra)


def body(fsdp_count, tensor_count, hidden, cotangent, documents, q_w, k_w, v_w, o_w, edge_weight):
    _, seqs, length, shard_cols = hidden.shape
    tokens = seqs * length
    model_width = shard_cols * tensor_count
    q_cols = q_w.shape[2]
    heads = q_cols // HD
    tensor_at, fsdp_at = lax.axis_index("tensor"), lax.axis_index("fsdp")
    share = tensor_count // fsdp_count
    home = tensor_at // share == fsdp_at
    par = (tensor_at % share).astype(jnp.int32).reshape(1)
    other = functools.partial(passed_along, axis="fsdp", by=1)
    flip = lambda block: swapped(block, tensor_count)
    far_flip = lambda block: lax.ppermute(
        block, "tensor", [(t, (t + share) % tensor_count) for t in range(tensor_count)]
    )

    shard = hidden[0].reshape(tokens, shard_cols)
    cotan = cotangent[0].reshape(tokens, shard_cols)
    h_near, h_far = spread(shard, fsdp_count, tensor_count)

    wide = shard.astype(F32)
    squares = jnp.sum(wide * wide, -1)
    squares = squares + flip(squares)
    got_x = far_flip(squares)
    docs = documents[0].astype(F32)
    got_y = other(jnp.concatenate([squares, docs.reshape(tokens)]))
    got_xy = lax.ppermute(
        squares,
        ("fsdp", "tensor"),
        [
            (g * tensor_count + t, (1 - g) * tensor_count + (t + share) % tensor_count)
            for g in range(fsdp_count)
            for t in range(tensor_count)
        ],
    )
    w_proj = jnp.concatenate(after((k_w[0], v_w[0], q_w[0]), squares), 1).astype(BF16)
    w_out = after(o_w[0], squares).astype(BF16)
    tables = rope_tables(length, HD)
    positions = jnp.arange(length)
    causal = (positions[:, None] >= positions[None, :])[None]

    def mask_of(docs):
        return (causal & (docs[:, :, None] == docs[:, None, :])).astype(F32)

    mask = mask_of(after(docs, squares))
    got_x, w_proj, w_out, mask, *tables = lax.optimization_barrier(
        (got_x, w_proj, w_out, mask, *tables)
    )
    inv_own = lax.rsqrt((squares + got_x) / model_width + norm_eps)
    inv_oth = lax.rsqrt((got_y[:tokens] + got_xy) / model_width + norm_eps)

    def pieces_of(part, near, far, scale_own=None, scale_oth=None):
        own = jnp.where(home, part, near)
        oth = jnp.where(home, near, far)
        if scale_own is not None:
            own = (own.astype(F32) * scale_own[:, None]).astype(BF16)
            oth = (oth.astype(F32) * scale_oth[:, None]).astype(BF16)
        mine = lax.optimization_barrier(jnp.stack([own, oth]))
        return mine, flip(mine)

    c_near, c_far = spread(after(cotan, h_near, h_far), fsdp_count, tensor_count)
    h_pieces = pieces_of(shard, h_near, h_far, inv_own, inv_oth)
    first_cols, rest_cols = 3 * HD, q_cols - HD
    first_own, first_oth, first_sent = project(par, h_pieces, w_proj, 0, first_cols)
    first_got = other(first_sent)
    rest_own, rest_oth, rest_sent = project(par, after(h_pieces, first_sent), w_proj, 1, rest_cols)
    mask_oth = mask_of(after(got_y[tokens:], rest_sent).reshape(docs.shape))
    edge = after(edge_weight, first_sent)
    coef = jnp.concatenate([passed_along(edge, "gossip", 1), edge_weight])
    c_near, c_far = after((c_near, c_far), rest_sent, mask_oth, coef)
    c_pieces = []
    for i in range(CORE_PARTS):
        at = slice(i * tokens // CORE_PARTS, (i + 1) * tokens // CORE_PARTS)
        c_pieces += pieces_of(cotan[at], c_near[at], c_far[at])
    first_got = after(first_got, *c_pieces[::2])
    first = functools.partial(
        per_sequence, first_kernel, tables=tables, outs=(HD,) * 4, name="first_head", work=4
    )
    q0, key, value, ctx0 = first((first_own, (first_got, 0)), mask=mask)
    q0_oth, key_oth, value_oth, ctx0_oth = first((first_oth, (first_got, 1)), mask=mask_oth)
    rest_got = other(after(rest_sent, first_got))

    def shared(pair, *gates):
        updated, sent = pair
        sent = after(sent, *gates) if gates else sent
        return updated, passed_along(sent, "gossip", 1), passed_along(sent, "gossip", -1)

    o_step = functools.partial(step_weights, par, c_pieces)
    blocks = shard_cols // BLOCK
    z1 = shared(o_step(ctx0, ctx0_oth, o_w[0], 0, HD, (0, blocks // 2)))
    z2 = shared(o_step(after(ctx0, z1[0]), ctx0_oth, o_w[0], 0, HD, (blocks // 2, blocks)))
    d_own, d_oth, d_sent = project(par, after(c_pieces, z2[0]), w_out, 0, q_cols)
    rest_got = after(rest_got, d_sent, *z1[1:])
    d_got = other(after(d_sent, rest_got))
    rest = functools.partial(
        per_sequence,
        functools.partial(rest_kernel, heads - 1),
        tables=tables,
        outs=(rest_cols,) * 2,
        name="rest_heads",
        work=4 * (heads - 1),
    )
    q_rest, ctx_rest = rest((rest_own, (rest_got, 0), key, value), mask=mask)
    q_rest_oth, ctx_rest_oth = rest(
        (rest_oth, (rest_got, 1), key_oth, value_oth), mask=mask_oth
    )
    chunks = [z1, z2]
    for i in range(heads - 1):
        at = slice(i * HD, (i + 1) * HD)
        d_ctx = after(ctx_rest[:, at], chunks[-1][0])
        chunks.append(shared(o_step(d_ctx, ctx_rest_oth[:, at], o_w[0], (i + 1) * HD, HD)))
    d_got = after(d_got, chunks[-1][0])
    back = functools.partial(
        per_sequence,
        functools.partial(back_kernel, heads),
        tables=tables,
        outs=(q_cols + 2 * HD,),
        name="attention_back",
        work=14 * heads,
    )
    d_proj = back((d_own, (d_got, 0), q0, q_rest, key, value), mask=mask)[0]
    d_proj_oth = back(
        (d_oth, (d_got, 1), q0_oth, q_rest_oth, key_oth, value_oth), mask=mask_oth
    )[0]
    h_step = functools.partial(step_weights, par, h_pieces)
    for weight, first_col, begin, cols in (
        (k_w[0], 0, 0, HD),
        (v_w[0], 0, HD, HD),
        *((q_w[0], i * HD, (i + 2) * HD, HD) for i in range(heads)),
    ):
        at = slice(begin, begin + cols)
        d_own = after(d_proj[:, at], chunks[-1][0])
        chunks.append(shared(h_step(d_own, d_proj_oth[:, at], weight, first_col, cols)))

    outs = {}
    last = coef
    for chunk, (name, cols, width, first_col) in zip(
        chunks,
        [("o", HD, q_cols, max(i, 0) * HD) for i in range(-1, heads)]
        + [("k", HD, HD, 0), ("v", HD, HD, 0), *(("q", HD, q_cols, i * HD) for i in range(heads))],
    ):
        chunk = (chunk[0], *after(chunk[1:], last))
        begin = blocks // 2 if chunk[0].shape[1] < shard_cols and name in outs else 0
        last = outs[name] = mix(
            par, coef, chunk, shard_cols, cols, width, first_col, begin, outs.get(name)
        )
    return tuple(outs[name][None] for name in "qkvo")


def solution(mesh):
    fsdp_count, tensor_count = mesh.shape["fsdp"], mesh.shape["tensor"]
    assert fsdp_count == 2 and tensor_count == 2 * fsdp_count
    activations = P("gossip", "fsdp", None, "tensor")
    weights = P("gossip", "fsdp", "tensor")
    return jax.shard_map(
        functools.partial(body, fsdp_count, tensor_count),
        mesh=mesh,
        in_specs=(activations, activations, P("gossip", "fsdp", None))
        + (weights,) * 4
        + (P("gossip"),),
        out_specs=(weights,) * 4,
        check_vma=False,
    )
```

```python
import functools
import math

import jax
import jax.numpy as jnp
from jax import lax
from jax.experimental import pallas as pl
from jax.experimental.pallas import tpu as pltpu
from jax.sharding import PartitionSpec as P

HD = 128
F32 = jnp.float32
BF16 = jnp.bfloat16
BLOCK = 256
CORE_PARTS = 4
VMEM_LIMIT = 24 * 1024 * 1024

rope_theta = 500000.0
learn_rate = 0.001
norm_eps = 1e-05

NN = (((1,), (0,)), ((), ()))
NT = (((1,), (1,)), ((), ()))
TN = (((0,), (0,)), ((), ()))


def mm(left, right, form=NN):
    return lax.dot_general(left, right, form, preferred_element_type=F32)


def cost(flops, bytes_accessed, transcendentals=0):
    return pl.CostEstimate(
        flops=int(flops), bytes_accessed=int(bytes_accessed), transcendentals=int(transcendentals)
    )


def params(count):
    return pltpu.CompilerParams(
        dimension_semantics=("arbitrary",) * count, vmem_limit_bytes=VMEM_LIMIT
    )


def passed_along(shard, axis, by):
    count = lax.axis_size(axis)
    return lax.ppermute(shard, axis, [(i, (i + by) % count) for i in range(count)])


def rope_tables(length, head_size):
    half_dim = head_size // 2
    positions = jnp.arange(length, dtype=F32)
    freqs = jnp.exp(jnp.arange(half_dim, dtype=F32) * (-2.0 / head_size * math.log(rope_theta)))
    angles = positions[:, None] * freqs[None, :]
    cosine, sine = jnp.cos(angles), jnp.sin(angles)
    return jnp.concatenate([cosine, cosine], 1), jnp.concatenate([-sine, sine], 1)


def after(value, *others):
    return lax.optimization_barrier((value, *others))[0]


def spread(shard, fsdp_count, tensor_count):
    share = tensor_count // fsdp_count
    near, far = [], []
    for g in range(fsdp_count):
        for t in range(tensor_count):
            x, lane = divmod(t, share)
            source = g * tensor_count + t
            across = x * tensor_count + (1 - x) * share + lane
            if x == g:
                near.append((source, across))
            else:
                near.append((source, x * tensor_count + t))
                far.append((source, across))
    axes = ("fsdp", "tensor")
    return lax.ppermute(shard, axes, near), lax.ppermute(shard, axes, far)


def swapped(block, tensor_count):
    return lax.ppermute(block, "tensor", [(t, t ^ 1) for t in range(tensor_count)])


def parity_halves(par_ref, w_ref, rows):
    par = par_ref[0]
    return (
        w_ref[pl.ds(pl.multiple_of(par * rows, rows), rows), :],
        w_ref[pl.ds(pl.multiple_of((1 - par) * rows, rows), rows), :],
    )


def project_kernel(par_ref, *refs):
    *pieces, w_ref, sum_ref, sent_ref = refs
    _, tokens, rows = pieces[0].shape
    w_mine, w_theirs = parity_halves(par_ref, w_ref, rows)
    for part in range(len(pieces) // 2):
        mine, theirs = pieces[2 * part : 2 * part + 2]
        at = pl.ds(part * tokens, tokens)
        other = mm(mine[1], w_mine) + mm(theirs[1], w_theirs)
        sent_ref[0, at, :] = other.astype(BF16)
        sum_ref[1, at, :] = other
        own = mm(mine[0], w_mine) + mm(theirs[0], w_theirs)
        sent_ref[1, at, :] = own.astype(BF16)
        sum_ref[0, at, :] = own


def project(par, pieces, weight, at, cols):
    parts = len(pieces) // 2
    _, tokens, rows = pieces[0].shape
    if parts == 1:
        steps, unit = 2, cols
        piece = pl.BlockSpec((2, tokens // steps, rows), lambda i, p: (0, i, 0))
        whole = pl.BlockSpec((2 * rows, cols), lambda i, p: (0, at))
        out = pl.BlockSpec((2, tokens // steps, cols), lambda i, p: (0, i, 0))
    else:
        unit = 2 * HD
        steps = cols // unit
        piece = pl.BlockSpec((2, tokens, rows), lambda i, p: (0, 0, 0))
        whole = pl.BlockSpec((2 * rows, unit), lambda i, p: (0, at * steps + i))
        out = pl.BlockSpec((2, parts * tokens, unit), lambda i, p: (0, 0, i))
    tokens = tokens * parts
    return pl.pallas_call(
        project_kernel,
        grid_spec=pltpu.PrefetchScalarGridSpec(
            num_scalar_prefetch=1,
            grid=(steps,),
            in_specs=[piece] * len(pieces) + [whole],
            out_specs=[out, out],
        ),
        out_shape=[jax.ShapeDtypeStruct((2, tokens, cols), kind) for kind in (F32, BF16)],
        compiler_params=params(1),
        cost_estimate=cost(8 * tokens * rows * cols, 8 * tokens * rows + 10 * tokens * cols),
        name="project",
    )(par, *pieces, weight)


def rotated(values, cos, sin):
    return values * cos + pltpu.roll(values, HD // 2, 1) * sin


def unrotated(values, cos, sin):
    return values * cos - pltpu.roll(values, HD // 2, 1) * sin


def probabilities(query, key, mask):
    scores = mm(query, key, NT) * (1.0 / math.sqrt(HD))
    exp_scores = jnp.where(mask, jnp.exp(scores), 0.0)
    return exp_scores / jnp.sum(exp_scores, -1, keepdims=True)


def first_kernel(own, oth, cos, sin, mask, q_ref, k_ref, v_ref, ctx_ref):
    proj = own[...] + oth[...].astype(F32)
    key = rotated(proj[:, :HD], cos[...], sin[...]).astype(BF16)
    value = proj[:, HD : 2 * HD].astype(BF16)
    query = rotated(proj[:, 2 * HD :], cos[...], sin[...]).astype(BF16)
    probs = probabilities(query, key, mask[0] > 0.5)
    ctx_ref[...] = mm(probs.astype(BF16), value).astype(BF16)
    q_ref[...] = query
    k_ref[...] = key
    v_ref[...] = value


def rest_kernel(heads, own, oth, cos, sin, mask, k_ref, v_ref, q_ref, ctx_ref):
    key, value = k_ref[...], v_ref[...]
    allowed = mask[0] > 0.5
    for head in range(heads):
        cols = slice(head * HD, (head + 1) * HD)
        proj = own[:, cols] + oth[:, cols].astype(F32)
        query = rotated(proj, cos[...], sin[...]).astype(BF16)
        probs = probabilities(query, key, allowed)
        ctx_ref[:, cols] = mm(probs.astype(BF16), value).astype(BF16)
        q_ref[:, cols] = query


def back_kernel(
    heads, own, oth, cos, sin, mask, q0_ref, q_ref, k_ref, v_ref, out_ref
):
    key, value = k_ref[...], v_ref[...]
    allowed = mask[0] > 0.5
    d_key = jnp.zeros(key.shape, F32)
    d_value = jnp.zeros(key.shape, F32)
    for head in range(heads):
        cols = slice(head * HD, (head + 1) * HD)
        query = q0_ref[...] if head == 0 else q_ref[:, (head - 1) * HD : head * HD]
        d_out = (own[:, cols] + oth[:, cols].astype(F32)).astype(BF16)
        probs = probabilities(query, key, allowed)
        d_probs = mm(d_out, value, NT)
        d_value += mm(probs.astype(BF16), d_out, TN)
        delta = jnp.sum(probs * d_probs, -1, keepdims=True)
        d_scores = (probs * (d_probs - delta) * (1.0 / math.sqrt(HD))).astype(BF16)
        d_query = unrotated(mm(d_scores, key), cos[...], sin[...])
        out_ref[:, (head + 2) * HD : (head + 3) * HD] = d_query.astype(BF16)
        d_key += mm(d_scores, query, TN)
    out_ref[:, :HD] = unrotated(d_key, cos[...], sin[...]).astype(BF16)
    out_ref[:, HD : 2 * HD] = d_value.astype(BF16)


def per_sequence(kernel, arrays, *, tables, mask, outs, name, work):
    length = tables[0].shape[0]
    groups, seqs = mask.shape[:2]

    def by_rows(cols):
        return pl.BlockSpec((None, length, cols), lambda g, s: (g, s, 0))

    specs = [by_rows(a.shape[2]) for a in arrays]
    table = pl.BlockSpec((length, HD), lambda g, s: (0, 0))
    square = pl.BlockSpec((None, 1, length, length), lambda g, s: (g, s, 0, 0))
    return pl.pallas_call(
        kernel,
        grid=(groups, seqs),
        in_specs=specs[:2] + [table, table, square] + specs[2:],
        out_specs=[by_rows(cols) for cols in outs],
        out_shape=[jax.ShapeDtypeStruct((groups, seqs * length, cols), BF16) for cols in outs],
        compiler_params=params(2),
        cost_estimate=cost(
            groups * seqs * work * length * length * HD,
            4 * groups * seqs * length * sum(outs),
            groups * seqs * length * length,
        ),
        name=name,
    )(*arrays[:2], *tables, mask, *arrays[2:])


def step_kernel(par_ref, *refs):
    *pieces, dy, w_mine, w_theirs, u_ref, sent_ref = refs
    cols = u_ref.shape[2]
    tokens = pieces[0].shape[1]
    at = pl.ds(pl.multiple_of(pl.program_id(1) * cols, cols), cols)
    for place, weight in ((0, w_mine), (1, w_theirs)):
        grad = 0.0
        for group in range(2):
            term = 0.0
            for part in range(len(pieces) // 2):
                rows = pl.ds(part * tokens, tokens)
                term += mm(pieces[2 * part + place][group], dy[group, rows, at], TN)
            grad += term.astype(BF16).astype(F32)
        updated = weight[...] - learn_rate * grad
        u_ref[place] = updated
        sent_ref[place] = updated.astype(BF16)


def step_weights(par, pieces, d_both, d_col, cols, weight, first_col, unit, blocks=None):
    _, part_tokens, rows = pieces[0].shape
    tokens = d_both.shape[1]
    d_at = d_col // cols
    total = rows // BLOCK
    begin, end = blocks or (0, total)
    count = end - begin
    at = first_col // unit
    piece = pl.BlockSpec((2, part_tokens, BLOCK), lambda j, k, p: (0, 0, begin + j))
    whole = pl.BlockSpec((2, tokens, cols), lambda j, k, p: (0, 0, d_at))
    out = pl.BlockSpec((2, BLOCK, unit), lambda j, k, p: (0, j, k))
    mine = lambda j, k, p: (p[0] * total + begin + j, at + k)
    theirs = lambda j, k, p: ((1 - p[0]) * total + begin + j, at + k)
    return pl.pallas_call(
        step_kernel,
        grid_spec=pltpu.PrefetchScalarGridSpec(
            num_scalar_prefetch=1,
            grid=(count, cols // unit),
            in_specs=[piece] * len(pieces)
            + [whole]
            + [pl.BlockSpec((BLOCK, unit), mine), pl.BlockSpec((BLOCK, unit), theirs)],
            out_specs=[out, out],
        ),
        out_shape=[
            jax.ShapeDtypeStruct((2, count * BLOCK, cols), F32),
            jax.ShapeDtypeStruct((2, count * BLOCK, cols), BF16),
        ],
        compiler_params=params(2),
        cost_estimate=cost(8 * tokens * count * BLOCK * cols, count * BLOCK * (8 * tokens + 20 * cols)),
        name="step_weights",
    )(par, *pieces, d_both, weight, weight)


def mix_kernel(par_ref, coef, u_ref, low_ref, high_ref, *outs):
    updated = u_ref[0]
    out_ref = outs[-1]
    out_ref[...] = (
        updated
        + coef[0] * (low_ref[0].astype(F32) - updated)
        + coef[1] * (high_ref[0].astype(F32) - updated)
    )


def mix(par, coef, chunk, rows, cols, width, to_col, begin, buffer=None):
    count = chunk[0].shape[1]
    block = min(4 * BLOCK, count)
    total, first, to = rows // block, begin * BLOCK // block, to_col // cols
    source = pl.BlockSpec((1, block, cols), lambda i, j, p: (i, j, 0))
    place = pl.BlockSpec(
        (block, cols), lambda i, j, p: ((p[0] + i * (1 - 2 * p[0])) * total + first + j, to)
    )
    extra = [] if buffer is None else [buffer]
    return pl.pallas_call(
        mix_kernel,
        grid_spec=pltpu.PrefetchScalarGridSpec(
            num_scalar_prefetch=1,
            grid=(2, count // block),
            in_specs=[pl.BlockSpec(memory_space=pltpu.SMEM), source, source, source]
            + [pl.BlockSpec(memory_space=pl.ANY)] * len(extra),
            out_specs=place,
        ),
        out_shape=jax.ShapeDtypeStruct((2 * rows, width), F32),
        input_output_aliases={5: 0} if extra else {},
        compiler_params=params(2),
        cost_estimate=cost(10 * count * cols, 24 * count * cols),
        name="mix",
    )(par, coef, *chunk, *extra)


def body(fsdp_count, tensor_count, hidden, cotangent, documents, q_w, k_w, v_w, o_w, edge_weight):
    _, seqs, length, shard_cols = hidden.shape
    tokens = seqs * length
    model_width = shard_cols * tensor_count
    q_cols = q_w.shape[2]
    heads = q_cols // HD
    tensor_at, fsdp_at = lax.axis_index("tensor"), lax.axis_index("fsdp")
    share = tensor_count // fsdp_count
    home = tensor_at // share == fsdp_at
    par = (tensor_at % share).astype(jnp.int32).reshape(1)
    other = functools.partial(passed_along, axis="fsdp", by=1)
    flip = lambda block: swapped(block, tensor_count)
    far_flip = lambda block: lax.ppermute(
        block, "tensor", [(t, (t + share) % tensor_count) for t in range(tensor_count)]
    )

    shard = hidden[0].reshape(tokens, shard_cols)
    cotan = cotangent[0].reshape(tokens, shard_cols)
    h_near, h_far = spread(shard, fsdp_count, tensor_count)

    wide = shard.astype(F32)
    squares = jnp.sum(wide * wide, -1)
    squares = squares + flip(squares)
    got_x = far_flip(squares)
    docs = documents[0].astype(F32)
    got_y = other(jnp.concatenate([squares, docs.reshape(tokens)]))
    got_xy = lax.ppermute(
        squares,
        ("fsdp", "tensor"),
        [
            (g * tensor_count + t, (1 - g) * tensor_count + (t + share) % tensor_count)
            for g in range(fsdp_count)
            for t in range(tensor_count)
        ],
    )
    w_proj = jnp.concatenate(after((k_w[0], v_w[0], q_w[0]), squares), 1).astype(BF16)
    w_out = after(o_w[0], squares).astype(BF16)
    tables = rope_tables(length, HD)
    positions = jnp.arange(length)
    causal = (positions[:, None] >= positions[None, :])[None]

    def mask_of(docs):
        return (causal & (docs[:, :, None] == docs[:, None, :])).astype(F32)

    got_x, w_proj, w_out, *tables = lax.optimization_barrier((got_x, w_proj, w_out, *tables))
    inv_own = lax.rsqrt((squares + got_x) / model_width + norm_eps)
    inv_oth = lax.rsqrt((got_y[:tokens] + got_xy) / model_width + norm_eps)

    def pieces_of(part, near, far, scale_own=None, scale_oth=None):
        own = jnp.where(home, part, near)
        oth = jnp.where(home, near, far)
        if scale_own is not None:
            own = (own.astype(F32) * scale_own[:, None]).astype(BF16)
            oth = (oth.astype(F32) * scale_oth[:, None]).astype(BF16)
        mine = lax.optimization_barrier(jnp.stack([own, oth]))
        return mine, flip(mine)

    c_near, c_far = spread(after(cotan, h_near, h_far), fsdp_count, tensor_count)
    h_pieces = pieces_of(shard, h_near, h_far, inv_own, inv_oth)
    first_cols, rest_cols = 3 * HD, q_cols - HD
    first_sum, first_sent = project(par, h_pieces, w_proj, 0, first_cols)
    first_got = other(first_sent)
    rest_sum, rest_sent = project(par, after(h_pieces, first_sent), w_proj, 1, rest_cols)
    mask = jnp.stack(
        [mask_of(after(both, rest_sent)) for both in (docs, got_y[tokens:].reshape(docs.shape))]
    )
    edge = after(edge_weight, first_sent)
    coef = jnp.concatenate([passed_along(edge, "gossip", 1), edge_weight])
    c_near, c_far = after((c_near, c_far), rest_sent, mask, coef)
    c_pieces = []
    for i in range(CORE_PARTS):
        at = slice(i * tokens // CORE_PARTS, (i + 1) * tokens // CORE_PARTS)
        c_pieces += pieces_of(cotan[at], c_near[at], c_far[at])
    first_got = after(first_got, *c_pieces[::2])
    attend = functools.partial(per_sequence, tables=tables, mask=mask)
    q0, key, value, ctx0 = attend(
        first_kernel, (first_sum, first_got), outs=(HD,) * 4, name="first_head", work=4
    )
    rest_got = other(after(rest_sent, first_got))

    def shared(pair, *gates):
        updated, sent = pair
        sent = after(sent, *gates) if gates else sent
        return updated, passed_along(sent, "gossip", 1), passed_along(sent, "gossip", -1)

    o_step = functools.partial(step_weights, par, c_pieces)
    blocks = shard_cols // BLOCK
    z1 = shared(o_step(ctx0, 0, HD, o_w[0], 0, HD, (0, blocks // 2)))
    z2 = shared(o_step(after(ctx0, z1[0]), 0, HD, o_w[0], 0, HD, (blocks // 2, blocks)))
    d_sum, d_sent = project(par, after(c_pieces, z2[0]), w_out, 0, q_cols)
    rest_got = after(rest_got, d_sent, *z1[1:])
    d_got = other(after(d_sent, rest_got))
    q_rest, ctx_rest = attend(
        functools.partial(rest_kernel, heads - 1),
        (rest_sum, rest_got, key, value),
        outs=(rest_cols,) * 2,
        name="rest_heads",
        work=4 * (heads - 1),
    )
    chunks = [z1, z2]
    for i in range(heads - 1):
        d_ctx = after(ctx_rest, chunks[-1][0], *(z2[1:] if i == 1 else ()))
        chunks.append(shared(o_step(d_ctx, i * HD, HD, o_w[0], (i + 1) * HD, HD)))
    d_got = after(d_got, chunks[-1][0])
    d_proj = attend(
        functools.partial(back_kernel, heads),
        (d_sum, d_got, q0, q_rest, key, value),
        outs=(q_cols + 2 * HD,),
        name="attention_back",
        work=14 * heads,
    )[0]
    h_step = functools.partial(step_weights, par, h_pieces)
    for i, (weight, first_col) in enumerate(
        ((k_w[0], 0), (v_w[0], 0), *((q_w[0], i * HD) for i in range(heads)))
    ):
        d_both = after(d_proj, chunks[-1][0])
        chunks.append(shared(h_step(d_both, i * HD, HD, weight, first_col, HD)))

    outs = {}
    last = coef
    for chunk, (name, cols, width, first_col) in zip(
        chunks,
        [("o", HD, q_cols, max(i, 0) * HD) for i in range(-1, heads)]
        + [("k", HD, HD, 0), ("v", HD, HD, 0), *(("q", HD, q_cols, i * HD) for i in range(heads))],
    ):
        chunk = (chunk[0], *after(chunk[1:], last))
        begin = blocks // 2 if chunk[0].shape[1] < shard_cols and name in outs else 0
        last = outs[name] = mix(
            par, coef, chunk, shard_cols, cols, width, first_col, begin, outs.get(name)
        )
    return tuple(outs[name][None] for name in "qkvo")


def solution(mesh):
    fsdp_count, tensor_count = mesh.shape["fsdp"], mesh.shape["tensor"]
    assert fsdp_count == 2 and tensor_count == 2 * fsdp_count
    activations = P("gossip", "fsdp", None, "tensor")
    weights = P("gossip", "fsdp", "tensor")
    return jax.shard_map(
        functools.partial(body, fsdp_count, tensor_count),
        mesh=mesh,
        in_specs=(activations, activations, P("gossip", "fsdp", None))
        + (weights,) * 4
        + (P("gossip"),),
        out_specs=(weights,) * 4,
        check_vma=False,
    )
```

```python
import functools
import math

import jax
import jax.numpy as jnp
from jax import lax
from jax.experimental import pallas as pl
from jax.experimental.pallas import tpu as pltpu
from jax.sharding import PartitionSpec as P

HD = 128
F32 = jnp.float32
BF16 = jnp.bfloat16
BLOCK = 256
CORE_PARTS = 4
VMEM_LIMIT = 24 * 1024 * 1024

rope_theta = 500000.0
learn_rate = 0.001
norm_eps = 1e-05

NN = (((1,), (0,)), ((), ()))
NT = (((1,), (1,)), ((), ()))
TN = (((0,), (0,)), ((), ()))


def mm(left, right, form=NN):
    return lax.dot_general(left, right, form, preferred_element_type=F32)


def cost(flops, bytes_accessed, transcendentals=0):
    return pl.CostEstimate(
        flops=int(flops), bytes_accessed=int(bytes_accessed), transcendentals=int(transcendentals)
    )


def params(count):
    return pltpu.CompilerParams(
        dimension_semantics=("arbitrary",) * count, vmem_limit_bytes=VMEM_LIMIT
    )


def passed_along(shard, axis, by):
    count = lax.axis_size(axis)
    return lax.ppermute(shard, axis, [(i, (i + by) % count) for i in range(count)])


def rope_tables(length, head_size):
    half_dim = head_size // 2
    positions = jnp.arange(length, dtype=F32)
    freqs = jnp.exp(jnp.arange(half_dim, dtype=F32) * (-2.0 / head_size * math.log(rope_theta)))
    angles = positions[:, None] * freqs[None, :]
    cosine, sine = jnp.cos(angles), jnp.sin(angles)
    return jnp.concatenate([cosine, cosine], 1), jnp.concatenate([-sine, sine], 1)


def after(value, *others):
    return lax.optimization_barrier((value, *others))[0]


def spread(shard, fsdp_count, tensor_count):
    share = tensor_count // fsdp_count
    near, far = [], []
    for g in range(fsdp_count):
        for t in range(tensor_count):
            x, lane = divmod(t, share)
            source = g * tensor_count + t
            across = x * tensor_count + (1 - x) * share + lane
            if x == g:
                near.append((source, across))
            else:
                near.append((source, x * tensor_count + t))
                far.append((source, across))
    axes = ("fsdp", "tensor")
    return lax.ppermute(shard, axes, near), lax.ppermute(shard, axes, far)


def swapped(block, tensor_count):
    return lax.ppermute(block, "tensor", [(t, t ^ 1) for t in range(tensor_count)])


def parity_halves(par_ref, w_ref, rows):
    par = par_ref[0]
    return (
        w_ref[pl.ds(pl.multiple_of(par * rows, rows), rows), :],
        w_ref[pl.ds(pl.multiple_of((1 - par) * rows, rows), rows), :],
    )


def project_kernel(par_ref, *refs):
    *pieces, w_ref, sum_ref, sent_ref = refs
    _, tokens, rows = pieces[0].shape
    w_mine, w_theirs = parity_halves(par_ref, w_ref, rows)
    for part in range(len(pieces) // 2):
        mine, theirs = pieces[2 * part : 2 * part + 2]
        at = pl.ds(part * tokens, tokens)
        other = mm(mine[1], w_mine) + mm(theirs[1], w_theirs)
        sent_ref[0, at, :] = other.astype(BF16)
        sum_ref[1, at, :] = other
        own = mm(mine[0], w_mine) + mm(theirs[0], w_theirs)
        sent_ref[1, at, :] = own.astype(BF16)
        sum_ref[0, at, :] = own


def project(par, pieces, weight, at, cols):
    parts = len(pieces) // 2
    _, tokens, rows = pieces[0].shape
    if parts == 1:
        steps, unit = 2, cols
        piece = pl.BlockSpec((2, tokens // steps, rows), lambda i, p: (0, i, 0))
        whole = pl.BlockSpec((2 * rows, cols), lambda i, p: (0, at))
        out = pl.BlockSpec((2, tokens // steps, cols), lambda i, p: (0, i, 0))
    else:
        unit = 2 * HD
        steps = cols // unit
        piece = pl.BlockSpec((2, tokens, rows), lambda i, p: (0, 0, 0))
        whole = pl.BlockSpec((2 * rows, unit), lambda i, p: (0, at * steps + i))
        out = pl.BlockSpec((2, parts * tokens, unit), lambda i, p: (0, 0, i))
    tokens = tokens * parts
    return pl.pallas_call(
        project_kernel,
        grid_spec=pltpu.PrefetchScalarGridSpec(
            num_scalar_prefetch=1,
            grid=(steps,),
            in_specs=[piece] * len(pieces) + [whole],
            out_specs=[out, out],
        ),
        out_shape=[jax.ShapeDtypeStruct((2, tokens, cols), kind) for kind in (F32, BF16)],
        compiler_params=params(1),
        cost_estimate=cost(8 * tokens * rows * cols, 8 * tokens * rows + 10 * tokens * cols),
        name="project",
    )(par, *pieces, weight)


def rotated(values, cos, sin):
    return values * cos + pltpu.roll(values, HD // 2, 1) * sin


def unrotated(values, cos, sin):
    return values * cos - pltpu.roll(values, HD // 2, 1) * sin


def probabilities(query, key, mask):
    scores = mm(query, key, NT) * (1.0 / math.sqrt(HD))
    exp_scores = jnp.where(mask, jnp.exp(scores), 0.0)
    return exp_scores / jnp.sum(exp_scores, -1, keepdims=True)


def first_kernel(own, oth, cos, sin, mask, q_ref, k_ref, v_ref, ctx_ref):
    proj = own[...] + oth[...].astype(F32)
    key = rotated(proj[:, :HD], cos[...], sin[...]).astype(BF16)
    value = proj[:, HD : 2 * HD].astype(BF16)
    query = rotated(proj[:, 2 * HD :], cos[...], sin[...]).astype(BF16)
    probs = probabilities(query, key, mask[0] > 0.5)
    ctx_ref[...] = mm(probs.astype(BF16), value).astype(BF16)
    q_ref[...] = query
    k_ref[...] = key
    v_ref[...] = value


def rest_kernel(heads, own, oth, cos, sin, mask, k_ref, v_ref, q_ref, ctx_ref):
    key, value = k_ref[...], v_ref[...]
    allowed = mask[0] > 0.5
    for head in range(heads):
        cols = slice(head * HD, (head + 1) * HD)
        proj = own[:, cols] + oth[:, cols].astype(F32)
        query = rotated(proj, cos[...], sin[...]).astype(BF16)
        probs = probabilities(query, key, allowed)
        ctx_ref[:, cols] = mm(probs.astype(BF16), value).astype(BF16)
        q_ref[:, cols] = query


def back_kernel(
    heads, own, oth, cos, sin, mask, q0_ref, q_ref, k_ref, v_ref, out_ref
):
    key, value = k_ref[...], v_ref[...]
    allowed = mask[0] > 0.5
    d_key = jnp.zeros(key.shape, F32)
    d_value = jnp.zeros(key.shape, F32)
    for head in range(heads):
        cols = slice(head * HD, (head + 1) * HD)
        query = q0_ref[...] if head == 0 else q_ref[:, (head - 1) * HD : head * HD]
        d_out = (own[:, cols] + oth[:, cols].astype(F32)).astype(BF16)
        probs = probabilities(query, key, allowed)
        d_probs = mm(d_out, value, NT)
        d_value += mm(probs.astype(BF16), d_out, TN)
        delta = jnp.sum(probs * d_probs, -1, keepdims=True)
        d_scores = (probs * (d_probs - delta) * (1.0 / math.sqrt(HD))).astype(BF16)
        d_query = unrotated(mm(d_scores, key), cos[...], sin[...])
        out_ref[:, (head + 2) * HD : (head + 3) * HD] = d_query.astype(BF16)
        d_key += mm(d_scores, query, TN)
    out_ref[:, :HD] = unrotated(d_key, cos[...], sin[...]).astype(BF16)
    out_ref[:, HD : 2 * HD] = d_value.astype(BF16)


def per_sequence(kernel, arrays, *, tables, mask, outs, name, work):
    length = tables[0].shape[0]
    groups, seqs = mask.shape[:2]

    def by_rows(cols):
        return pl.BlockSpec((None, length, cols), lambda g, s: (g, s, 0))

    specs = [by_rows(a.shape[2]) for a in arrays]
    table = pl.BlockSpec((length, HD), lambda g, s: (0, 0))
    square = pl.BlockSpec((None, 1, length, length), lambda g, s: (g, s, 0, 0))
    return pl.pallas_call(
        kernel,
        grid=(groups, seqs),
        in_specs=specs[:2] + [table, table, square] + specs[2:],
        out_specs=[by_rows(cols) for cols in outs],
        out_shape=[jax.ShapeDtypeStruct((groups, seqs * length, cols), BF16) for cols in outs],
        compiler_params=params(2),
        cost_estimate=cost(
            groups * seqs * work * length * length * HD,
            4 * groups * seqs * length * sum(outs),
            groups * seqs * length * length,
        ),
        name=name,
    )(*arrays[:2], *tables, mask, *arrays[2:])


def step_kernel(par_ref, *refs):
    *pieces, dy, w_mine, w_theirs, u_ref, sent_ref = refs
    cols = u_ref.shape[2]
    tokens = pieces[0].shape[1]
    at = pl.ds(pl.multiple_of(pl.program_id(1) * cols, cols), cols)
    for place, weight in ((0, w_mine), (1, w_theirs)):
        grad = 0.0
        for group in range(2):
            term = 0.0
            for part in range(len(pieces) // 2):
                rows = pl.ds(part * tokens, tokens)
                term += mm(pieces[2 * part + place][group], dy[group, rows, at], TN)
            grad += term.astype(BF16).astype(F32)
        updated = weight[...] - learn_rate * grad
        u_ref[place] = updated
        sent_ref[place] = updated.astype(BF16)


def step_weights(par, pieces, d_both, d_col, cols, weight, first_col, unit, blocks=None):
    _, part_tokens, rows = pieces[0].shape
    tokens = d_both.shape[1]
    d_at = d_col // cols
    total = rows // BLOCK
    begin, end = blocks or (0, total)
    count = end - begin
    at = first_col // unit
    piece = pl.BlockSpec((2, part_tokens, BLOCK), lambda j, k, p: (0, 0, begin + j))
    whole = pl.BlockSpec((2, tokens, cols), lambda j, k, p: (0, 0, d_at))
    out = pl.BlockSpec((2, BLOCK, unit), lambda j, k, p: (0, j, k))
    mine = lambda j, k, p: (p[0] * total + begin + j, at + k)
    theirs = lambda j, k, p: ((1 - p[0]) * total + begin + j, at + k)
    return pl.pallas_call(
        step_kernel,
        grid_spec=pltpu.PrefetchScalarGridSpec(
            num_scalar_prefetch=1,
            grid=(count, cols // unit),
            in_specs=[piece] * len(pieces)
            + [whole]
            + [pl.BlockSpec((BLOCK, unit), mine), pl.BlockSpec((BLOCK, unit), theirs)],
            out_specs=[out, out],
        ),
        out_shape=[
            jax.ShapeDtypeStruct((2, count * BLOCK, cols), F32),
            jax.ShapeDtypeStruct((2, count * BLOCK, cols), BF16),
        ],
        compiler_params=params(2),
        cost_estimate=cost(8 * tokens * count * BLOCK * cols, count * BLOCK * (8 * tokens + 20 * cols)),
        name="step_weights",
    )(par, *pieces, d_both, weight, weight)


def mix_kernel(par_ref, coef, u_ref, low_ref, high_ref, *outs):
    updated = u_ref[0]
    out_ref = outs[-1]
    out_ref[...] = (
        updated
        + coef[0] * (low_ref[0].astype(F32) - updated)
        + coef[1] * (high_ref[0].astype(F32) - updated)
    )


def mix(par, coef, chunk, rows, cols, width, to_col, begin, buffer=None):
    count = chunk[0].shape[1]
    block = min(4 * BLOCK, count)
    total, first, to = rows // block, begin * BLOCK // block, to_col // cols
    source = pl.BlockSpec((1, block, cols), lambda i, j, p: (i, j, 0))
    place = pl.BlockSpec(
        (block, cols), lambda i, j, p: ((p[0] + i * (1 - 2 * p[0])) * total + first + j, to)
    )
    extra = [] if buffer is None else [buffer]
    return pl.pallas_call(
        mix_kernel,
        grid_spec=pltpu.PrefetchScalarGridSpec(
            num_scalar_prefetch=1,
            grid=(2, count // block),
            in_specs=[pl.BlockSpec(memory_space=pltpu.SMEM), source, source, source]
            + [pl.BlockSpec(memory_space=pl.ANY)] * len(extra),
            out_specs=place,
        ),
        out_shape=jax.ShapeDtypeStruct((2 * rows, width), F32),
        input_output_aliases={5: 0} if extra else {},
        compiler_params=params(2),
        cost_estimate=cost(10 * count * cols, 24 * count * cols),
        name="mix",
    )(par, coef, *chunk, *extra)


def body(fsdp_count, tensor_count, hidden, cotangent, documents, q_w, k_w, v_w, o_w, edge_weight):
    _, seqs, length, shard_cols = hidden.shape
    tokens = seqs * length
    model_width = shard_cols * tensor_count
    q_cols = q_w.shape[2]
    heads = q_cols // HD
    tensor_at, fsdp_at = lax.axis_index("tensor"), lax.axis_index("fsdp")
    share = tensor_count // fsdp_count
    home = tensor_at // share == fsdp_at
    par = (tensor_at % share).astype(jnp.int32).reshape(1)
    other = functools.partial(passed_along, axis="fsdp", by=1)
    flip = lambda block: swapped(block, tensor_count)
    far_flip = lambda block: lax.ppermute(
        block, "tensor", [(t, (t + share) % tensor_count) for t in range(tensor_count)]
    )

    shard = hidden[0].reshape(tokens, shard_cols)
    cotan = cotangent[0].reshape(tokens, shard_cols)
    h_near, h_far = spread(shard, fsdp_count, tensor_count)

    wide = shard.astype(F32)
    squares = jnp.sum(wide * wide, -1)
    squares = squares + flip(squares)
    got_x = far_flip(squares)
    docs = documents[0].astype(F32)
    got_y = other(jnp.concatenate([squares, docs.reshape(tokens)]))
    got_xy = lax.ppermute(
        squares,
        ("fsdp", "tensor"),
        [
            (g * tensor_count + t, (1 - g) * tensor_count + (t + share) % tensor_count)
            for g in range(fsdp_count)
            for t in range(tensor_count)
        ],
    )
    w_proj = jnp.concatenate(after((k_w[0], v_w[0], q_w[0]), squares), 1).astype(BF16)
    w_out = after(o_w[0], squares).astype(BF16)
    tables = rope_tables(length, HD)
    positions = jnp.arange(length)
    causal = (positions[:, None] >= positions[None, :])[None]

    def mask_of(docs):
        return (causal & (docs[:, :, None] == docs[:, None, :])).astype(F32)

    got_x, w_proj, w_out, *tables = lax.optimization_barrier((got_x, w_proj, w_out, *tables))
    inv_own = lax.rsqrt((squares + got_x) / model_width + norm_eps)
    inv_oth = lax.rsqrt((got_y[:tokens] + got_xy) / model_width + norm_eps)

    def pieces_of(part, near, far, scale_own=None, scale_oth=None):
        own = jnp.where(home, part, near)
        oth = jnp.where(home, near, far)
        if scale_own is not None:
            own = (own.astype(F32) * scale_own[:, None]).astype(BF16)
            oth = (oth.astype(F32) * scale_oth[:, None]).astype(BF16)
        mine = lax.optimization_barrier(jnp.stack([own, oth]))
        return mine, flip(mine)

    c_near, c_far = spread(after(cotan, h_near, h_far), fsdp_count, tensor_count)
    h_pieces = pieces_of(shard, h_near, h_far, inv_own, inv_oth)
    first_cols, rest_cols = 3 * HD, q_cols - HD
    first_sum, first_sent = project(par, h_pieces, w_proj, 0, first_cols)
    first_got = other(first_sent)
    rest_sum, rest_sent = project(par, after(h_pieces, first_sent), w_proj, 1, rest_cols)
    mask = jnp.stack(
        [mask_of(after(both, rest_sent)) for both in (docs, got_y[tokens:].reshape(docs.shape))]
    )
    edge = after(edge_weight, first_sent)
    coef = jnp.concatenate([passed_along(edge, "gossip", 1), edge_weight])
    c_near, c_far = after((c_near, c_far), rest_sent, mask, coef)
    c_pieces = []
    for i in range(CORE_PARTS):
        at = slice(i * tokens // CORE_PARTS, (i + 1) * tokens // CORE_PARTS)
        c_pieces += pieces_of(cotan[at], c_near[at], c_far[at])
    first_got = after(first_got, *c_pieces[::2])
    attend = functools.partial(per_sequence, tables=tables, mask=mask)
    q0, key, value, ctx0 = attend(
        first_kernel, (first_sum, first_got), outs=(HD,) * 4, name="first_head", work=4
    )
    rest_got = other(after(rest_sent, ctx0))

    def shared(pair, *gates):
        updated, sent = pair
        sent = after(sent, *gates) if gates else sent
        return updated, passed_along(sent, "gossip", 1), passed_along(sent, "gossip", -1)

    o_step = functools.partial(step_weights, par, c_pieces)
    blocks = shard_cols // BLOCK
    z1 = shared(o_step(ctx0, 0, HD, o_w[0], 0, HD, (0, blocks // 2)))
    z2 = shared(o_step(after(ctx0, z1[0]), 0, HD, o_w[0], 0, HD, (blocks // 2, blocks)))
    d_sum, d_sent = project(par, after(c_pieces, z2[0]), w_out, 0, q_cols)
    rest_got = after(rest_got, d_sent, *z1[1:])
    d_got = other(after(d_sent, rest_got))
    q_rest, ctx_rest = attend(
        functools.partial(rest_kernel, heads - 1),
        (rest_sum, rest_got, key, value),
        outs=(rest_cols,) * 2,
        name="rest_heads",
        work=4 * (heads - 1),
    )
    chunks = [z1, z2]
    for i in range(heads - 1):
        d_ctx = after(ctx_rest, chunks[-1][0], *(z2[1:] if i == 1 else ()))
        chunks.append(shared(o_step(d_ctx, i * HD, HD, o_w[0], (i + 1) * HD, HD)))
    d_got = after(d_got, chunks[-1][0])
    d_proj = attend(
        functools.partial(back_kernel, heads),
        (d_sum, d_got, q0, q_rest, key, value),
        outs=(q_cols + 2 * HD,),
        name="attention_back",
        work=14 * heads,
    )[0]
    h_step = functools.partial(step_weights, par, h_pieces)
    for i, (weight, first_col) in enumerate(
        ((k_w[0], 0), (v_w[0], 0), *((q_w[0], i * HD) for i in range(heads)))
    ):
        d_both = after(d_proj, chunks[-1][0])
        chunks.append(shared(h_step(d_both, i * HD, HD, weight, first_col, HD)))

    outs = {}
    last = coef
    for chunk, (name, cols, width, first_col) in zip(
        chunks,
        [("o", HD, q_cols, max(i, 0) * HD) for i in range(-1, heads)]
        + [("k", HD, HD, 0), ("v", HD, HD, 0), *(("q", HD, q_cols, i * HD) for i in range(heads))],
    ):
        chunk = (chunk[0], *after(chunk[1:], last))
        begin = blocks // 2 if chunk[0].shape[1] < shard_cols and name in outs else 0
        last = outs[name] = mix(
            par, coef, chunk, shard_cols, cols, width, first_col, begin, outs.get(name)
        )
    return tuple(outs[name][None] for name in "qkvo")


def solution(mesh):
    fsdp_count, tensor_count = mesh.shape["fsdp"], mesh.shape["tensor"]
    assert fsdp_count == 2 and tensor_count == 2 * fsdp_count
    activations = P("gossip", "fsdp", None, "tensor")
    weights = P("gossip", "fsdp", "tensor")
    return jax.shard_map(
        functools.partial(body, fsdp_count, tensor_count),
        mesh=mesh,
        in_specs=(activations, activations, P("gossip", "fsdp", None))
        + (weights,) * 4
        + (P("gossip"),),
        out_specs=(weights,) * 4,
        check_vma=False,
    )
```
